256 devices in a mesh: tm: 32 (over x, y, core), neur: 8 (over z).
Axes of the slice: x: 4, y: 4, z: 8, core: 2. Of those that a mesh axis runs over, the one named last changes fastest.
Arguments:
- activity: bfloat16 [51200, 12288], P('neur', 'tm'), may hold values from 0.01 to 1001, as said below
- patterns: bfloat16 [51200, 512], P('neur'), may hold values from 6.25e-05 to 0.08125, as said below
- loadings: bfloat16 [32, 12288], P(None, 'tm'), may hold values from 0.01 to 4.4, as said below
Outputs:
- h_next: float32 [32, 12288], P(None, 'tm')
- w_next: float32 [51200, 512], P(('neur', 'tm'))
- misfit: float32 [12288], P('tm')
The draws below stay inside these ranges and needn't reach their ends.
Inputs may be any that keep to these rules, and one draw needn't show every extreme that they name: `activity`: positive. `patterns`: positive. `loadings`: positive.
All inputs are finite; a program needn't handle non-finite values.
Results may differ from the reference program's by a relative error of at most 0.0009.
Values may be sent and summed in bfloat16 or wider, within the bound.
A program may use at most 128 MiB of HBM per device.

```python
import math
import jax
import jax.numpy as jnp
from jax import lax

NEURONS = 51200
RANK = 32
LAGS = 16
TIMEBINS = 12288
N_NEUR = 8


def draw_activity(key, part):
    rate_key, level_key, event_key, floor_key, amp_key = jax.random.split(jax.random.fold_in(key, 7), 5)
    shape = (NEURONS, TIMEBINS)
    neuron_ramp = jnp.exp(math.log(3.0) * (jnp.arange(NEURONS, dtype=jnp.float32)[:, None] / NEURONS - 0.5))
    time_ramp = jnp.exp(math.log(3.0) * (jnp.arange(TIMEBINS, dtype=jnp.float32)[None, :] / TIMEBINS - 0.5))
    rate = jnp.exp(jax.random.uniform(rate_key, (NEURONS, 1), jnp.float32, math.log(0.0005), math.log(0.004))) * neuron_ramp
    events = jax.random.uniform(event_key, shape, jnp.float32) < rate
    level = jnp.exp(jax.random.uniform(level_key, (NEURONS, 1), jnp.float32, math.log(0.05), math.log(0.5)))
    floor = level * jnp.exp(jax.random.uniform(floor_key, shape, jnp.float32, math.log(0.2), math.log(2.0)))
    amplitude = jnp.exp(jax.random.uniform(amp_key, shape, jnp.float32, math.log(20.0), math.log(577.0)))
    value = floor + jnp.where(events, amplitude * time_ramp, jnp.float32(0.0))
    return value.astype(jnp.bfloat16)


def draw_patterns(key, part):
    first_key, second_key, third_key = jax.random.split(key, 3)
    shape = (NEURONS, LAGS * RANK)
    base = jnp.exp(jax.random.uniform(first_key, shape, jnp.float32, math.log(0.1), 0.0))
    rowscale = jnp.exp(jax.random.uniform(third_key, (NEURONS, 1), jnp.float32, math.log(0.5), math.log(1.5)))
    column = jnp.exp(jax.random.uniform(second_key, (1, LAGS * RANK), jnp.float32, math.log(0.2), math.log(2.0)))
    ramp = jnp.exp(math.log(3.0) * (jnp.arange(NEURONS, dtype=jnp.float32)[:, None] / NEURONS - 0.5))
    overall = 8.0 / (LAGS * RANK)
    return (base * column * rowscale * ramp * overall).astype(jnp.bfloat16)


def draw_loadings(key, part):
    first_key, second_key = jax.random.split(key, 2)
    shape = (RANK, TIMEBINS)
    base = jnp.exp(jax.random.uniform(first_key, shape, jnp.float32, math.log(0.05), 0.0))
    factor_scale = jnp.exp(jax.random.uniform(second_key, (RANK, 1), jnp.float32, math.log(0.4), math.log(2.5)))
    ramp = jnp.exp(math.log(3.0) * (jnp.arange(TIMEBINS, dtype=jnp.float32)[None, :] / TIMEBINS - 0.5))
    return (base * factor_scale * ramp).astype(jnp.bfloat16)


def setup_inputs(seed: int = 0) -> dict:
    key_list = jax.random.split(jax.random.key(seed), 4)
    return {
        "activity": draw_activity(jax.random.fold_in(key_list[3], 71), 0),
        "patterns": draw_patterns(jax.random.fold_in(key_list[3], 71), 0),
        "loadings": draw_loadings(jax.random.fold_in(key_list[3], 71), 0),
    }


def lag_stack(factor, rim):
    extended = jnp.concatenate([rim, factor], axis=1)
    width = factor.shape[1]
    rows = [extended[:, LAGS - 1 - lag: LAGS - 1 - lag + width] for lag in range(LAGS)]
    return jnp.concatenate(rows, axis=0)


def reference(activity, patterns, loadings):
    zero_rim = jnp.zeros((RANK, LAGS - 1), loadings.dtype)
    block = NEURONS // N_NEUR
    acts = activity.reshape(N_NEUR, block, TIMEBINS)
    pats = patterns.reshape(N_NEUR, block, LAGS * RANK)
    stacked = lag_stack(loadings, zero_rim)

    def first(total, pair):
        act, pat = pair
        recon = jnp.dot(pat, stacked, preferred_element_type=jnp.float32)
        ratio = (act.astype(jnp.float32) / recon).astype(jnp.bfloat16)
        extended = jnp.concatenate([ratio, jnp.zeros((block, LAGS - 1), ratio.dtype)], axis=1)
        gram = lax.dot_general(pat, extended, (((0,), (0,)), ((), ())), preferred_element_type=jnp.float32)
        return total + gram, None

    gram, _ = lax.scan(first, jnp.zeros((LAGS * RANK, TIMEBINS + LAGS - 1), jnp.float32), (acts, pats))
    layered = gram.reshape(LAGS, RANK, TIMEBINS + LAGS - 1)
    numer = layered[0, :, 0:TIMEBINS]
    for lag in range(1, LAGS):
        numer = numer + layered[lag, :, lag:lag + TIMEBINS]
    colsum = jnp.sum(jnp.sum(patterns.astype(jnp.float32), axis=0).reshape(LAGS, RANK), axis=0)
    h_next = loadings.astype(jnp.float32) * numer / colsum[:, None]
    fresh = h_next.astype(jnp.bfloat16)
    stacked2 = lag_stack(fresh, zero_rim)
    lagsum = jnp.sum(stacked2.astype(jnp.float32), axis=1)

    def second(pair):
        act, pat = pair
        act32 = act.astype(jnp.float32)
        recon2 = jnp.dot(pat, stacked2, preferred_element_type=jnp.float32)
        diverge = jnp.sum(act32 * jnp.log(act32 / recon2) - act32 + recon2, axis=0)
        mass = jnp.sum(act32, axis=0)
        ratio2 = (act32 / recon2).astype(jnp.bfloat16)
        pnum = lax.dot_general(ratio2, stacked2, (((1,), (1,)), ((), ())), preferred_element_type=jnp.float32)
        return pat.astype(jnp.float32) * pnum / lagsum[None, :], diverge, mass

    w_blocks, diverges, masses = lax.map(second, (acts, pats))
    w_next = w_blocks.reshape(NEURONS, LAGS * RANK)
    misfit = jnp.sum(diverges, axis=0) / jnp.sum(masses, axis=0)
    return h_next, w_next, misfit
```

```python
import jax
import jax.numpy as jnp
from jax import lax
from jax.experimental import pallas as pl
from jax.experimental.pallas import tpu as pltpu
from jax.sharding import PartitionSpec as P

RANK = 32
LAGS = 16
NX = 4
NY = 4
NZ = 8
NTM = 32
ROWS = 6400
SPAN = 384
HALO = 128
EXT = HALO + SPAN
WIDTH = RANK * LAGS
CHUNKS = NX * NY
CROWS = ROWS // CHUNKS
OWN = CROWS // 2
PADDED = OWN + 8
TILE = 1280
TILES = ROWS // TILE
F32 = jnp.float32
BF16 = jnp.bfloat16
MESH = pl.DeviceIdType.MESH

ORDER = (
    (2, 2), (2, 1), (1, 2), (2, 3), (3, 2), (2, 0), (0, 2), (1, 1),
    (3, 3), (1, 3), (3, 1), (1, 0), (0, 1), (3, 0), (0, 3), (0, 0),
)
WHERE = {pair: i for i, pair in enumerate(ORDER)}


def coded(axis, start):
    return sum(ORDER[start + i][axis] << (2 * i) for i in range(8))


def relative(i):
    i = jnp.int32(i) if isinstance(i, int) else i
    low = i < 8
    shift = 2 * (i % 8)
    codes = [jnp.where(low, coded(axis, 0), coded(axis, 8)) for axis in (0, 1)]
    return [lax.shift_right_logical(code, shift) & 3 for code in codes]


H1L, H2L, H1R, H2R = 0, 8, 16, 24
C1L, C2L, C1R, C2R = 32, 34, 36, 38
PAIR = 40
ZRS, ZAG, ZMF = 56, 63, 70
LHALO, NHALO, HPAIR = 77, 78, 80
NSEM = 81


def dot(a, b):
    return jnp.dot(a, b, preferred_element_type=F32)


def shifted_rows(ext, lag):
    moved = ext if lag == 0 else pltpu.roll(ext, lag, 1)
    return moved[:, HALO:]


def kernel(
    act_hbm, pat_hbm, load_ref, h_ref, w_ref, mis_ref,
    act, pat, stack, stack_t, ratios, gram, lhalo, blocks, nhalo, ext_load, part, zrecv, hz, hz_pair,
    rat, prat, chunks, h1l, h2l, h1r, h2r, c1l, c2l, c1r, c2r, sums, zsums, lag8,
    isem, ssem, rsem,
):
    tm = lax.axis_index("tm")
    z = lax.axis_index("neur")
    x, y, c = tm // (2 * NY), (tm // 2) % NY, tm % 2

    def at(gx, gy):
        return (gx % NX) * (2 * NY) + (gy % NY) * 2 + c

    after, before = (tm + 1) % NTM, (tm + NTM - 1) % NTM
    partner = tm + 1 - 2 * c
    xp, xm, yp, ym = at(x + 1, y), at(x + 3, y), at(x, y + 1), at(x, y + 3)

    def remote(src, dst, number, to_tm, to_z):
        return pltpu.make_async_remote_copy(
            src_ref=src, dst_ref=dst, send_sem=ssem.at[number], recv_sem=rsem.at[number],
            device_id=(to_tm, to_z), device_id_type=MESH,
        )

    def loads(j):
        rows = pl.ds(pl.multiple_of(j * TILE, TILE), TILE)
        return (
            pltpu.make_async_copy(pat_hbm.at[rows], pat.at[rows], isem.at[j, 0]),
            pltpu.make_async_copy(act_hbm.at[rows], act.at[rows], isem.at[j, 1]),
        )

    for j in range(TILES):
        for copy in loads(j):
            copy.start()

    barrier = pltpu.get_barrier_semaphore()
    peers = [(after, z), (before, z), (partner, z), (xp, z), (xm, z), (yp, z), (ym, z)]
    peers += [(tm, (z + d) % NZ) for d in range(1, NZ)]
    for peer in peers:
        pl.semaphore_signal(barrier, inc=1, device_id=peer, device_id_type=MESH)
    pl.semaphore_wait(barrier, len(peers))

    halo_copy = remote(load_ref.at[:, SPAN - HALO :], lhalo, LHALO, after, z)
    halo_copy.start()
    ratios[:, SPAN:] = jnp.ones((TILE, WIDTH - SPAN), BF16)
    gram[...] = jnp.zeros_like(gram)
    halo_copy.wait()
    rim = jnp.where(tm > 0, lhalo[...].astype(F32), 0.0)
    ext = jnp.concatenate([rim, load_ref[...].astype(F32)], axis=1)
    for p in range(NZ):
        ext_load[p] = ext[4 * p : 4 * p + 4]
    for lag in range(LAGS):
        stack[RANK * lag : RANK * (lag + 1)] = shifted_rows(ext, lag).astype(BF16)

    def first(j, carry):
        for copy in loads(j):
            copy.wait()
        rows = pl.ds(pl.multiple_of(j * TILE, TILE), TILE)
        recon = dot(pat[rows], stack[...])
        ratios[:, :SPAN] = (act[rows].astype(F32) / recon).astype(BF16)
        gram[...] += lax.dot_general(
            pat[rows], ratios[...], (((0,), (0,)), ((), ())), preferred_element_type=F32
        )
        return carry

    lax.fori_loop(0, TILES, first, 0)

    lane = lax.broadcasted_iota(jnp.int32, (RANK, HALO), 1)
    numer = jnp.zeros((RANK, EXT), F32)
    colsum = jnp.zeros((RANK, HALO), F32)
    for lag in range(LAGS):
        rows = gram[RANK * lag : RANK * (lag + 1)]
        wide = jnp.concatenate([jnp.zeros((RANK, HALO), F32), rows[:, :SPAN]], axis=1)
        numer = numer + (wide if lag == 0 else pltpu.roll(wide, EXT - lag, 1))
        colsum = colsum + rows[:, SPAN:]
    blocks[0] = numer[:, :HALO]
    blocks[1] = numer[:, EXT - HALO :]
    to_before = remote(blocks.at[0], nhalo.at[0], NHALO, before, z)
    to_after = remote(blocks.at[1], nhalo.at[1], NHALO + 1, after, z)
    to_before.start()
    to_after.start()
    to_before.wait()
    to_after.wait()
    reach = lane >= HALO - (LAGS - 1)
    from_after = jnp.where(reach & (tm < NTM - 1), nhalo[0], 0.0)
    from_before = jnp.where(reach & (tm > 0), nhalo[1], 0.0)
    head = jnp.where(lane < 64, colsum, numer[:, :HALO] + from_before)
    tail = numer[:, EXT - HALO :] + from_after
    numer = jnp.concatenate([head, numer[:, HALO : EXT - HALO], tail], axis=1)
    for p in range(NZ):
        part[p] = numer[4 * p : 4 * p + 4]

    def over_z(src, dst, base):
        return [remote(src(d), dst(d), base + d - 1, tm, (z + d) % NZ) for d in range(1, NZ)]

    scatter = over_z(lambda d: part.at[(z + d) % NZ], lambda d: zrecv.at[d - 1], ZRS)
    for copy in scatter:
        copy.start()
    for copy in scatter:
        copy.wait()
    total = part[z]
    for d in range(1, NZ):
        total = total + zrecv[d - 1]
    hz[z] = ext_load[z] * total / total[:, 0:1]
    gather = over_z(lambda d: hz.at[z], lambda d: hz.at[z], ZAG)
    for copy in gather:
        copy.start()
    for copy in gather:
        copy.wait()
    to_partner = remote(hz, hz_pair, HPAIR, partner, z)
    to_partner.start()

    def fresh_of(ref):
        return jnp.concatenate([ref[p] for p in range(NZ)], axis=0)

    h_ext = fresh_of(hz)
    h_ref[...] = h_ext[:, HALO:]

    def put_stack(full, direct, first_row):
        full = full.astype(BF16).astype(F32)
        for group in range(LAGS // 4):
            rows = [shifted_rows(full, 4 * group + k) for k in range(4)]
            block = jnp.concatenate(rows, axis=0)
            if direct:
                stack[4 * RANK * group : 4 * RANK * (group + 1)] = block.astype(BF16)
            turned = block.T
            stack_t[first_row : first_row + SPAN, HALO * group : HALO * (group + 1)] = turned.astype(BF16)
            lag_rows = jnp.broadcast_to(jnp.sum(turned, axis=0, keepdims=True), (8, HALO))
            if direct:
                lag8[group] = lag_rows
            else:
                lag8[group] = lag8[group] + lag_rows

    put_stack(h_ext, True, 0)
    sums[...] = jnp.zeros_like(sums)

    def pair_copy(i):
        return remote(rat.at[1 - c, i], prat.at[i], PAIR + i, partner, z)

    def make_ratio(i):
        dx, dy = relative(i)
        start = (((x + dx) % NX) * NY + (y + dy) % NY) * CROWS
        rows = pl.ds(pl.multiple_of(start, 16), CROWS)
        wide = act[rows].astype(F32)
        recon = dot(pat[rows], stack[...])
        ratio = wide / recon
        diverge = wide * jnp.log(ratio) - wide + recon
        sums[0] += jnp.sum(diverge.reshape(CROWS // 8, 8, SPAN), axis=0)
        sums[1] += jnp.sum(wide.reshape(CROWS // 8, 8, SPAN), axis=0)
        rat[0, i] = ratio[:OWN].astype(BF16)
        rat[1, i] = ratio[OWN:].astype(BF16)
        pair_copy(i).start()

    make_ratio(0)
    to_partner.wait()
    put_stack(fresh_of(hz_pair), False, SPAN)


    def half(i, step, other, block, base1, base2, recv1, recv2, plus, minus):
        @pl.when(step == 2)
        def _():
            remote(chunks.at[i, block], recv1.at[other, 0], base1 + 2 * other, plus, z).start()
            remote(chunks.at[i, block + 1], recv1.at[other, 1], base1 + 2 * other + 1, minus, z).start()

        for k, (when, to) in enumerate(((1, plus), (3, minus))):

            @pl.when(step == when)
            def _():
                came = remote(chunks.at[i, block], recv1.at[other, k], base1 + 2 * other + k, to, z)
                came.wait_recv()
                chunks[i, block + k] += recv1[other, k]
                remote(
                    chunks.at[i, pl.ds(block, 2)], recv2.at[other, k], base2 + 2 * other + k, to, z
                ).start()

    def make_chunk(i):
        dx, dy = relative(i)
        pair_copy(i).wait_recv()
        made = dot(rat[c, i], stack_t[:SPAN]) + dot(prat[i], stack_t[SPAN:])
        for b in range(4):
            chunks[i, b, :OWN] = made[:, HALO * b : HALO * (b + 1)]
            chunks[i, b, OWN:] = lag8[b]
        half(i, dx, dy, 0, H1L, H2L, h1l, h2l, xp, xm)
        half(i, dy, dx, 2, H1R, H2R, h1r, h2r, yp, ym)

    def second(i, carry):
        make_ratio(i + 1)
        make_chunk(i)
        return carry

    lax.fori_loop(0, CHUNKS - 1, second, 0)

    diverge = jnp.sum(sums[0], axis=0, keepdims=True)
    mass = jnp.sum(sums[1], axis=0, keepdims=True)
    row = lax.broadcasted_iota(jnp.int32, (8, SPAN), 0)
    zsums[0] = jnp.where(row == 0, diverge, mass)
    spread = over_z(lambda d: zsums.at[0], lambda d: zsums.at[d], ZMF)
    for copy in spread:
        copy.start()

    make_chunk(CHUNKS - 1)

    def last_stage(pos, block, base2, recv2, cb1, cb2, crecv1, crecv2, plus, minus):
        def reduced(other):
            i = WHERE[pos(other)]
            for k in range(2):
                remote(
                    chunks.at[i, pl.ds(block, 2)], recv2.at[other, k], base2 + 2 * other + k, plus, z
                ).wait_recv()
            chunks[i, pl.ds(block, 2)] = chunks[i, pl.ds(block, 2)] + recv2[other, 0] + recv2[other, 1]
            return i

        def begin():
            i = reduced(2)
            remote(chunks.at[i, block], crecv1.at[0], cb1, plus, z).start()
            remote(chunks.at[i, block + 1], crecv1.at[1], cb1 + 1, minus, z).start()

        def middle():
            for k, (other, to) in enumerate(((1, plus), (3, minus))):
                i = reduced(other)
                remote(chunks.at[i, block], crecv1.at[k], cb1 + k, to, z).wait_recv()
                chunks[i, block + k] += crecv1[k]
                remote(chunks.at[i, pl.ds(block, 2)], crecv2.at[k], cb2 + k, to, z).start()

        def end():
            i = reduced(0)
            for k in range(2):
                remote(chunks.at[i, pl.ds(block, 2)], crecv2.at[k], cb2 + k, plus, z).wait_recv()
            chunks[i, pl.ds(block, 2)] = chunks[i, pl.ds(block, 2)] + crecv2[0] + crecv2[1]

        return begin, middle, end

    left = last_stage(lambda o: (0, o), 0, H2L, h2l, C1L, C2L, c1l, c2l, yp, ym)
    right = last_stage(lambda o: (o, 0), 2, H2R, h2r, C1R, C2R, c1r, c2r, xp, xm)
    for a, b in zip(left, right):
        a()
        b()

    mine = pl.ds(pl.multiple_of((x * NY + y) * CROWS, 16), CROWS)
    both = pat[mine].astype(F32)
    own = jnp.where(c == 0, both[:OWN], both[OWN:])
    for b in range(4):
        done = chunks[CHUNKS - 1, b]
        w_ref[:, HALO * b : HALO * (b + 1)] = own[:, HALO * b : HALO * (b + 1)] * done[:OWN] / done[OWN : OWN + 1]

    for copy in spread:
        copy.wait()
    everyone = zsums[0]
    for d in range(1, NZ):
        everyone = everyone + zsums[d]
    mis_ref[...] = everyone[0:1] / everyone[1:2]

    to_partner_done = [pair_copy(i) for i in range(CHUNKS)]
    for copy in to_partner_done:
        copy.wait_send()
    for base1, base2, recv1, recv2 in ((H1L, H2L, h1l, h2l), (H1R, H2R, h1r, h2r)):
        for other in range(4):
            for k in range(2):
                remote(chunks.at[0, 0], recv1.at[other, k], base1 + 2 * other + k, xp, z).wait_send()
                remote(chunks.at[0, pl.ds(0, 2)], recv2.at[other, k], base2 + 2 * other + k, xp, z).wait_send()
    for cb1, cb2, crecv1, crecv2 in ((C1L, C2L, c1l, c2l), (C1R, C2R, c1r, c2r)):
        for k in range(2):
            remote(chunks.at[0, 0], crecv1.at[k], cb1 + k, xp, z).wait_send()
            remote(chunks.at[0, pl.ds(0, 2)], crecv2.at[k], cb2 + k, xp, z).wait_send()


def body(activity, patterns, loadings):
    vmem = pl.BlockSpec(memory_space=pltpu.VMEM)
    anywhere = pl.BlockSpec(memory_space=pl.ANY)
    one = (PADDED, HALO)
    h_next, w_next, misfit = pl.pallas_call(
        kernel,
        out_shape=(
            jax.ShapeDtypeStruct((RANK, SPAN), F32),
            jax.ShapeDtypeStruct((OWN, WIDTH), F32),
            jax.ShapeDtypeStruct((1, SPAN), F32),
        ),
        in_specs=[anywhere, anywhere, vmem],
        out_specs=(vmem, vmem, vmem),
        scratch_shapes=[
            pltpu.VMEM((ROWS, SPAN), BF16),
            pltpu.VMEM((ROWS, WIDTH), BF16),
            pltpu.VMEM((WIDTH, SPAN), BF16),
            pltpu.VMEM((2 * SPAN, WIDTH), BF16),
            pltpu.VMEM((TILE, WIDTH), BF16),
            pltpu.VMEM((WIDTH, WIDTH), F32),
            pltpu.VMEM((RANK, HALO), BF16),
            pltpu.VMEM((2, RANK, HALO), F32),
            pltpu.VMEM((2, RANK, HALO), F32),
            pltpu.VMEM((NZ, 4, EXT), F32),
            pltpu.VMEM((NZ, 4, EXT), F32),
            pltpu.VMEM((NZ - 1, 4, EXT), F32),
            pltpu.VMEM((NZ, 4, EXT), F32),
            pltpu.VMEM((NZ, 4, EXT), F32),
            pltpu.VMEM((2, CHUNKS, OWN, SPAN), BF16),
            pltpu.VMEM((CHUNKS, OWN, SPAN), BF16),
            pltpu.VMEM((CHUNKS, 4) + one, F32),
            pltpu.VMEM((4, 2) + one, F32),
            pltpu.VMEM((4, 2, 2) + one, F32),
            pltpu.VMEM((4, 2) + one, F32),
            pltpu.VMEM((4, 2, 2) + one, F32),
            pltpu.VMEM((2,) + one, F32),
            pltpu.VMEM((2, 2) + one, F32),
            pltpu.VMEM((2,) + one, F32),
            pltpu.VMEM((2, 2) + one, F32),
            pltpu.VMEM((2, 8, SPAN), F32),
            pltpu.VMEM((NZ, 8, SPAN), F32),
            pltpu.VMEM((4, 8, HALO), F32),
            pltpu.SemaphoreType.DMA((TILES, 2)),
            pltpu.SemaphoreType.DMA((NSEM,)),
            pltpu.SemaphoreType.DMA((NSEM,)),
        ],
        compiler_params=pltpu.CompilerParams(
            collective_id=0, has_side_effects=True, vmem_limit_bytes=60 * 1024 * 1024
        ),
    )(activity, patterns, loadings)
    return h_next, w_next, misfit.reshape(SPAN)


def solution(mesh):
    return jax.shard_map(
        body,
        mesh=mesh,
        in_specs=(P("neur", "tm"), P("neur", None), P(None, "tm")),
        out_specs=(P(None, "tm"), P(("neur", "tm"), None), P("tm")),
        check_vma=False,
    )
```

```python
import jax
import jax.numpy as jnp
from jax import lax
from jax.experimental import pallas as pl
from jax.experimental.pallas import tpu as pltpu
from jax.sharding import PartitionSpec as P

RANK = 32
LAGS = 16
NX = 4
NY = 4
NZ = 8
NTM = 32
ROWS = 6400
SPAN = 384
HALO = 128
EXT = HALO + SPAN
WIDTH = RANK * LAGS
CHUNKS = NX * NY
CROWS = ROWS // CHUNKS
OWN = CROWS // 2
PADDED = OWN + 8
TILE = 1280
TILES = ROWS // TILE
EARLY = 9
F32 = jnp.float32
BF16 = jnp.bfloat16
MESH = pl.DeviceIdType.MESH

ORDER = (
    (2, 2), (2, 1), (1, 2), (2, 3), (3, 2), (2, 0), (0, 2), (1, 1),
    (3, 3), (1, 3), (3, 1), (1, 0), (0, 1), (3, 0), (0, 3), (0, 0),
)
WHERE = {pair: i for i, pair in enumerate(ORDER)}


def coded(axis, start):
    return sum(ORDER[start + i][axis] << (2 * i) for i in range(8))


def relative(i):
    i = jnp.int32(i) if isinstance(i, int) else i
    low = i < 8
    shift = 2 * (i % 8)
    codes = [jnp.where(low, coded(axis, 0), coded(axis, 8)) for axis in (0, 1)]
    return [lax.shift_right_logical(code, shift) & 3 for code in codes]


H1L, H2L, H1R, H2R = 0, 8, 16, 24
C1L, C2L, C1R, C2R = 32, 34, 36, 38
PAIR = 40
ZRS, ZAG, ZMF = 56, 63, 70
LHALO, NHALO, HPAIR = 77, 78, 80
NSEM = 81


def dot(a, b):
    return jnp.dot(a, b, preferred_element_type=F32)


def narrow(block):
    lag = block[OWN:]
    high = lag.astype(BF16).astype(F32)
    row = lax.broadcasted_iota(jnp.int32, (8, HALO), 0)
    return jnp.concatenate([block[:OWN], jnp.where(row < 4, high, lag - high)], axis=0).astype(BF16)


def widen(block):
    block = block.astype(F32)
    lag = block[OWN:]
    return jnp.concatenate([block[:OWN], lag + pltpu.roll(lag, 4, 0)], axis=0)


def shifted_rows(ext, lag):
    moved = ext if lag == 0 else pltpu.roll(ext, lag, 1)
    return moved[:, HALO:]


def kernel(
    act_hbm, pat_hbm, load_ref, h_ref, w_ref, mis_ref,
    act, pat, stack, stack_t, ratios, gram, lhalo, blocks, nhalo, ext_load, part, zrecv, hz, hz_pair,
    rat, prat, chunks, halved, h1l, h2l, h1r, h2r, c1l, c2l, c1r, c2r, sums, zsums, lag8,
    isem, ssem, rsem,
):
    tm = lax.axis_index("tm")
    z = lax.axis_index("neur")
    x, y, c = tm // (2 * NY), (tm // 2) % NY, tm % 2

    def at(gx, gy):
        return (gx % NX) * (2 * NY) + (gy % NY) * 2 + c

    after, before = (tm + 1) % NTM, (tm + NTM - 1) % NTM
    partner = tm + 1 - 2 * c
    xp, xm, yp, ym = at(x + 1, y), at(x + 3, y), at(x, y + 1), at(x, y + 3)

    def remote(src, dst, number, to_tm, to_z):
        return pltpu.make_async_remote_copy(
            src_ref=src, dst_ref=dst, send_sem=ssem.at[number], recv_sem=rsem.at[number],
            device_id=(to_tm, to_z), device_id_type=MESH,
        )

    def loads(j):
        rows = pl.ds(pl.multiple_of(j * TILE, TILE), TILE)
        return (
            pltpu.make_async_copy(pat_hbm.at[rows], pat.at[rows], isem.at[j, 0]),
            pltpu.make_async_copy(act_hbm.at[rows], act.at[rows], isem.at[j, 1]),
        )

    for j in range(TILES):
        for copy in loads(j):
            copy.start()

    barrier = pltpu.get_barrier_semaphore()
    peers = [(after, z), (before, z), (partner, z), (xp, z), (xm, z), (yp, z), (ym, z)]
    peers += [(tm, (z + d) % NZ) for d in range(1, NZ)]
    for peer in peers:
        pl.semaphore_signal(barrier, inc=1, device_id=peer, device_id_type=MESH)
    pl.semaphore_wait(barrier, len(peers))

    halo_copy = remote(load_ref.at[:, SPAN - HALO :], lhalo, LHALO, after, z)
    halo_copy.start()
    ratios[:, SPAN:] = jnp.ones((TILE, WIDTH - SPAN), BF16)
    gram[...] = jnp.zeros_like(gram)
    halo_copy.wait()
    rim = jnp.where(tm > 0, lhalo[...].astype(F32), 0.0)
    ext = jnp.concatenate([rim, load_ref[...].astype(F32)], axis=1)
    for p in range(NZ):
        ext_load[p] = ext[4 * p : 4 * p + 4]
    for lag in range(LAGS):
        stack[RANK * lag : RANK * (lag + 1)] = shifted_rows(ext, lag).astype(BF16)

    def first(j, carry):
        for copy in loads(j):
            copy.wait()
        rows = pl.ds(pl.multiple_of(j * TILE, TILE), TILE)
        recon = dot(pat[rows], stack[...])
        ratios[:, :SPAN] = (act[rows].astype(F32) / recon).astype(BF16)
        gram[...] += lax.dot_general(
            pat[rows], ratios[...], (((0,), (0,)), ((), ())), preferred_element_type=F32
        )
        return carry

    lax.fori_loop(0, TILES, first, 0)

    lane = lax.broadcasted_iota(jnp.int32, (RANK, HALO), 1)
    numer = jnp.zeros((RANK, EXT), F32)
    colsum = jnp.zeros((RANK, HALO), F32)
    for lag in range(LAGS):
        rows = gram[RANK * lag : RANK * (lag + 1)]
        wide = jnp.concatenate([jnp.zeros((RANK, HALO), F32), rows[:, :SPAN]], axis=1)
        numer = numer + (wide if lag == 0 else pltpu.roll(wide, EXT - lag, 1))
        colsum = colsum + rows[:, SPAN:]
    blocks[0] = numer[:, :HALO]
    blocks[1] = numer[:, EXT - HALO :]
    to_before = remote(blocks.at[0], nhalo.at[0], NHALO, before, z)
    to_after = remote(blocks.at[1], nhalo.at[1], NHALO + 1, after, z)
    to_before.start()
    to_after.start()
    to_before.wait()
    to_after.wait()
    reach = lane >= HALO - (LAGS - 1)
    from_after = jnp.where(reach & (tm < NTM - 1), nhalo[0], 0.0)
    from_before = jnp.where(reach & (tm > 0), nhalo[1], 0.0)
    head = jnp.where(lane < 64, colsum, numer[:, :HALO] + from_before)
    tail = numer[:, EXT - HALO :] + from_after
    numer = jnp.concatenate([head, numer[:, HALO : EXT - HALO], tail], axis=1)
    for p in range(NZ):
        part[p] = numer[4 * p : 4 * p + 4]

    def over_z(src, dst, base):
        return [remote(src(d), dst(d), base + d - 1, tm, (z + d) % NZ) for d in range(1, NZ)]

    scatter = over_z(lambda d: part.at[(z + d) % NZ], lambda d: zrecv.at[d - 1], ZRS)
    for copy in scatter:
        copy.start()
    for copy in scatter:
        copy.wait()
    total = part[z]
    for d in range(1, NZ):
        total = total + zrecv[d - 1]
    hz[z] = ext_load[z] * total / total[:, 0:1]
    gather = over_z(lambda d: hz.at[z], lambda d: hz.at[z], ZAG)
    for copy in gather:
        copy.start()
    for copy in gather:
        copy.wait()
    to_partner = remote(hz, hz_pair, HPAIR, partner, z)
    to_partner.start()

    def fresh_of(ref):
        return jnp.concatenate([ref[p] for p in range(NZ)], axis=0)

    h_ext = fresh_of(hz)
    h_ref[...] = h_ext[:, HALO:]

    def put_stack(full, direct, first_row):
        full = full.astype(BF16).astype(F32)
        for group in range(LAGS // 4):
            rows = [shifted_rows(full, 4 * group + k) for k in range(4)]
            block = jnp.concatenate(rows, axis=0)
            if direct:
                stack[4 * RANK * group : 4 * RANK * (group + 1)] = block.astype(BF16)
            turned = block.T
            stack_t[first_row : first_row + SPAN, HALO * group : HALO * (group + 1)] = turned.astype(BF16)
            lag_rows = jnp.broadcast_to(jnp.sum(turned, axis=0, keepdims=True), (8, HALO))
            if direct:
                lag8[group] = lag_rows
            else:
                lag8[group] = lag8[group] + lag_rows

    put_stack(h_ext, True, 0)
    sums[...] = jnp.zeros_like(sums)

    def pair_copy(i):
        return remote(rat.at[1 - c, i], prat.at[i], PAIR + i, partner, z)

    def make_ratio(i):
        dx, dy = relative(i)
        start = (((x + dx) % NX) * NY + (y + dy) % NY) * CROWS
        rows = pl.ds(pl.multiple_of(start, 16), CROWS)
        wide = act[rows].astype(F32)
        recon = dot(pat[rows], stack[...])
        ratio = wide / recon
        diverge = wide * jnp.log(ratio) - wide + recon
        sums[0] += jnp.sum(diverge.reshape(CROWS // 8, 8, SPAN), axis=0)
        sums[1] += jnp.sum(wide.reshape(CROWS // 8, 8, SPAN), axis=0)
        rat[0, i] = ratio[:OWN].astype(BF16)
        rat[1, i] = ratio[OWN:].astype(BF16)
        pair_copy(i).start()

    make_ratio(0)
    to_partner.wait()
    put_stack(fresh_of(hz_pair), False, SPAN)


    def half(i, step, other, block, base1, base2, recv1, recv2, plus, minus):
        @pl.when(step == 2)
        def _():
            for k, to in ((0, plus), (1, minus)):
                halved[i, block + k] = narrow(chunks[i, block + k])
                remote(halved.at[i, block + k], recv1.at[other, k], base1 + 2 * other + k, to, z).start()

        for k, (when, to) in enumerate(((1, plus), (3, minus))):

            @pl.when(step == when)
            def _():
                halved[i, block + 1 - k] = narrow(chunks[i, block + 1 - k])
                came = remote(halved.at[i, block], recv1.at[other, k], base1 + 2 * other + k, to, z)
                came.wait_recv()
                halved[i, block + k] = narrow(chunks[i, block + k] + widen(recv1[other, k]))
                remote(
                    halved.at[i, pl.ds(block, 2)], recv2.at[other, k], base2 + 2 * other + k, to, z
                ).start()

    def make_chunk(i):
        dx, dy = relative(i)
        pair_copy(i).wait_recv()
        made = dot(rat[c, i], stack_t[:SPAN]) + dot(prat[i], stack_t[SPAN:])
        for b in range(4):
            chunks[i, b, :OWN] = made[:, HALO * b : HALO * (b + 1)]
            chunks[i, b, OWN:] = lag8[b]
        half(i, dx, dy, 0, H1L, H2L, h1l, h2l, xp, xm)
        half(i, dy, dx, 2, H1R, H2R, h1r, h2r, yp, ym)

    def second(i, carry):
        make_ratio(i + 1)
        make_chunk(i)
        return carry

    def last_stage(pos, block, base2, recv2, cb1, cb2, crecv1, crecv2, plus, minus):
        def reduced(other):
            i = WHERE[pos(other)]
            for k in range(2):
                remote(
                    halved.at[i, pl.ds(block, 2)], recv2.at[other, k], base2 + 2 * other + k, plus, z
                ).wait_recv()
            for b in range(2):
                chunks[i, block + b] += widen(recv2[other, 0, b]) + widen(recv2[other, 1, b])
            return i

        def begin():
            i = reduced(2)
            remote(chunks.at[i, block], crecv1.at[0], cb1, plus, z).start()
            remote(chunks.at[i, block + 1], crecv1.at[1], cb1 + 1, minus, z).start()

        def middle():
            for k, (other, to) in enumerate(((1, plus), (3, minus))):
                i = reduced(other)
                remote(chunks.at[i, block], crecv1.at[k], cb1 + k, to, z).wait_recv()
                chunks[i, block + k] += crecv1[k]
                remote(chunks.at[i, pl.ds(block, 2)], crecv2.at[k], cb2 + k, to, z).start()

        def end():
            i = reduced(0)
            for k in range(2):
                remote(chunks.at[i, pl.ds(block, 2)], crecv2.at[k], cb2 + k, plus, z).wait_recv()
            chunks[i, pl.ds(block, 2)] = chunks[i, pl.ds(block, 2)] + crecv2[0] + crecv2[1]

        return begin, middle, end

    left = last_stage(lambda o: (0, o), 0, H2L, h2l, C1L, C2L, c1l, c2l, yp, ym)
    right = last_stage(lambda o: (o, 0), 2, H2R, h2r, C1R, C2R, c1r, c2r, xp, xm)
    lax.fori_loop(0, EARLY, second, 0)
    for begin in (left[0], right[0]):
        begin()
    lax.fori_loop(EARLY, CHUNKS - 1, second, 0)

    diverge = jnp.sum(sums[0], axis=0, keepdims=True)
    mass = jnp.sum(sums[1], axis=0, keepdims=True)
    row = lax.broadcasted_iota(jnp.int32, (8, SPAN), 0)
    zsums[0] = jnp.where(row == 0, diverge, mass)
    spread = over_z(lambda d: zsums.at[0], lambda d: zsums.at[d], ZMF)
    for copy in spread:
        copy.start()

    for middle in (left[1], right[1]):
        middle()
    make_chunk(CHUNKS - 1)
    for end in (left[2], right[2]):
        end()


    mine = pl.ds(pl.multiple_of((x * NY + y) * CROWS, 16), CROWS)
    both = pat[mine].astype(F32)
    own = jnp.where(c == 0, both[:OWN], both[OWN:])
    for b in range(4):
        done = chunks[CHUNKS - 1, b]
        w_ref[:, HALO * b : HALO * (b + 1)] = own[:, HALO * b : HALO * (b + 1)] * done[:OWN] / done[OWN : OWN + 1]

    for copy in spread:
        copy.wait()
    everyone = zsums[0]
    for d in range(1, NZ):
        everyone = everyone + zsums[d]
    mis_ref[...] = everyone[0:1] / everyone[1:2]

    to_partner_done = [pair_copy(i) for i in range(CHUNKS)]
    for copy in to_partner_done:
        copy.wait_send()
    for base1, base2, recv1, recv2 in ((H1L, H2L, h1l, h2l), (H1R, H2R, h1r, h2r)):
        for other in range(4):
            for k in range(2):
                remote(halved.at[0, 0], recv1.at[other, k], base1 + 2 * other + k, xp, z).wait_send()
                remote(halved.at[0, pl.ds(0, 2)], recv2.at[other, k], base2 + 2 * other + k, xp, z).wait_send()
    for cb1, cb2, crecv1, crecv2 in ((C1L, C2L, c1l, c2l), (C1R, C2R, c1r, c2r)):
        for k in range(2):
            remote(chunks.at[0, 0], crecv1.at[k], cb1 + k, xp, z).wait_send()
            remote(chunks.at[0, pl.ds(0, 2)], crecv2.at[k], cb2 + k, xp, z).wait_send()


def body(activity, patterns, loadings):
    vmem = pl.BlockSpec(memory_space=pltpu.VMEM)
    anywhere = pl.BlockSpec(memory_space=pl.ANY)
    one = (PADDED, HALO)
    h_next, w_next, misfit = pl.pallas_call(
        kernel,
        out_shape=(
            jax.ShapeDtypeStruct((RANK, SPAN), F32),
            jax.ShapeDtypeStruct((OWN, WIDTH), F32),
            jax.ShapeDtypeStruct((1, SPAN), F32),
        ),
        in_specs=[anywhere, anywhere, vmem],
        out_specs=(vmem, vmem, vmem),
        scratch_shapes=[
            pltpu.VMEM((ROWS, SPAN), BF16),
            pltpu.VMEM((ROWS, WIDTH), BF16),
            pltpu.VMEM((WIDTH, SPAN), BF16),
            pltpu.VMEM((2 * SPAN, WIDTH), BF16),
            pltpu.VMEM((TILE, WIDTH), BF16),
            pltpu.VMEM((WIDTH, WIDTH), F32),
            pltpu.VMEM((RANK, HALO), BF16),
            pltpu.VMEM((2, RANK, HALO), F32),
            pltpu.VMEM((2, RANK, HALO), F32),
            pltpu.VMEM((NZ, 4, EXT), F32),
            pltpu.VMEM((NZ, 4, EXT), F32),
            pltpu.VMEM((NZ - 1, 4, EXT), F32),
            pltpu.VMEM((NZ, 4, EXT), F32),
            pltpu.VMEM((NZ, 4, EXT), F32),
            pltpu.VMEM((2, CHUNKS, OWN, SPAN), BF16),
            pltpu.VMEM((CHUNKS, OWN, SPAN), BF16),
            pltpu.VMEM((CHUNKS, 4) + one, F32),
            pltpu.VMEM((CHUNKS, 4) + one, BF16),
            pltpu.VMEM((4, 2) + one, BF16),
            pltpu.VMEM((4, 2, 2) + one, BF16),
            pltpu.VMEM((4, 2) + one, BF16),
            pltpu.VMEM((4, 2, 2) + one, BF16),
            pltpu.VMEM((2,) + one, F32),
            pltpu.VMEM((2, 2) + one, F32),
            pltpu.VMEM((2,) + one, F32),
            pltpu.VMEM((2, 2) + one, F32),
            pltpu.VMEM((2, 8, SPAN), F32),
            pltpu.VMEM((NZ, 8, SPAN), F32),
            pltpu.VMEM((4, 8, HALO), F32),
            pltpu.SemaphoreType.DMA((TILES, 2)),
            pltpu.SemaphoreType.DMA((NSEM,)),
            pltpu.SemaphoreType.DMA((NSEM,)),
        ],
        compiler_params=pltpu.CompilerParams(
            collective_id=0, has_side_effects=True, vmem_limit_bytes=60 * 1024 * 1024
        ),
    )(activity, patterns, loadings)
    return h_next, w_next, misfit.reshape(SPAN)


def solution(mesh):
    return jax.shard_map(
        body,
        mesh=mesh,
        in_specs=(P("neur", "tm"), P("neur", None), P(None, "tm")),
        out_specs=(P(None, "tm"), P(("neur", "tm"), None), P("tm")),
        check_vma=False,
    )
```

```python
import jax
import jax.numpy as jnp
from jax import lax
from jax.experimental import pallas as pl
from jax.experimental.pallas import tpu as pltpu
from jax.sharding import PartitionSpec as P

RANK = 32
LAGS = 16
NX = 4
NY = 4
NZ = 8
NTM = 32
ROWS = 6400
SPAN = 384
HALO = 128
EXT = HALO + SPAN
WIDTH = RANK * LAGS
CHUNKS = NX * NY
CROWS = ROWS // CHUNKS
OWN = CROWS // 2
PADDED = OWN + 8
TILE = 1280
TILES = ROWS // TILE
EARLY = 9
LEAD = 3
F32 = jnp.float32
BF16 = jnp.bfloat16
MESH = pl.DeviceIdType.MESH

ORDER = (
    (2, 2), (2, 1), (1, 2), (2, 3), (3, 2), (2, 0), (0, 2), (1, 1),
    (3, 3), (1, 3), (3, 1), (1, 0), (0, 1), (3, 0), (0, 3), (0, 0),
)
WHERE = {pair: i for i, pair in enumerate(ORDER)}


def coded(axis, start):
    return sum(ORDER[start + i][axis] << (2 * i) for i in range(8))


def relative(i):
    i = jnp.int32(i) if isinstance(i, int) else i
    low = i < 8
    shift = 2 * (i % 8)
    codes = [jnp.where(low, coded(axis, 0), coded(axis, 8)) for axis in (0, 1)]
    return [lax.shift_right_logical(code, shift) & 3 for code in codes]


H1L, H2L, H1R, H2R = 0, 8, 16, 24
C1L, C2L, C1R, C2R = 32, 34, 36, 38
PAIR = 40
ZRS, ZAG, ZMF = 56, 63, 70
LHALO, NHALO, HPAIR = 77, 78, 80
EDGE = 81
NSEM = 97


def dot(a, b):
    return jnp.dot(a, b, preferred_element_type=F32)


def narrow(block):
    lag = block[OWN:]
    high = lag.astype(BF16).astype(F32)
    row = lax.broadcasted_iota(jnp.int32, (8, HALO), 0)
    return jnp.concatenate([block[:OWN], jnp.where(row < 4, high, lag - high)], axis=0).astype(BF16)


def widen(block):
    block = block.astype(F32)
    lag = block[OWN:]
    return jnp.concatenate([block[:OWN], lag + pltpu.roll(lag, 4, 0)], axis=0)


def shifted_rows(ext, lag):
    moved = ext if lag == 0 else pltpu.roll(ext, lag, 1)
    return moved[:, HALO:]


def kernel(
    act_hbm, pat_hbm, load_ref, h_ref, w_ref, mis_ref,
    act, pat, stack, stack_t, ratios, gram, lhalo, blocks, nhalo, ext_load, part, zrecv, hz, hz_pair,
    rat, prat, chunks, halved, h1l, h2l, h1r, h2r, c1l, c2l, c1r, c2r, sums, zsums, lag8,
    isem, ssem, rsem,
):
    tm = lax.axis_index("tm")
    z = lax.axis_index("neur")
    x, y, c = tm // (2 * NY), (tm // 2) % NY, tm % 2

    def at(gx, gy):
        return (gx % NX) * (2 * NY) + (gy % NY) * 2 + c

    after, before = (tm + 1) % NTM, (tm + NTM - 1) % NTM
    partner = tm + 1 - 2 * c
    xp, xm, yp, ym = at(x + 1, y), at(x + 3, y), at(x, y + 1), at(x, y + 3)

    def remote(src, dst, number, to_tm, to_z):
        return pltpu.make_async_remote_copy(
            src_ref=src, dst_ref=dst, send_sem=ssem.at[number], recv_sem=rsem.at[number],
            device_id=(to_tm, to_z), device_id_type=MESH,
        )

    def loads(j):
        rows = pl.ds(pl.multiple_of(j * TILE, TILE), TILE)
        return (
            pltpu.make_async_copy(pat_hbm.at[rows], pat.at[rows], isem.at[j, 0]),
            pltpu.make_async_copy(act_hbm.at[rows], act.at[rows], isem.at[j, 1]),
        )

    for j in range(TILES):
        for copy in loads(j):
            copy.start()

    barrier = pltpu.get_barrier_semaphore()
    peers = [(after, z), (before, z), (partner, z), (xp, z), (xm, z), (yp, z), (ym, z)]
    peers += [(to, (z + d) % NZ) for to in (tm, after, before) for d in range(1, NZ)]
    for peer in peers:
        pl.semaphore_signal(barrier, inc=1, device_id=peer, device_id_type=MESH)
    pl.semaphore_wait(barrier, len(peers))

    halo_copy = remote(load_ref.at[:, SPAN - HALO :], lhalo, LHALO, after, z)
    halo_copy.start()
    ratios[:, SPAN:] = jnp.ones((TILE, WIDTH - SPAN), BF16)
    gram[...] = jnp.zeros_like(gram)
    halo_copy.wait()
    rim = jnp.where(tm > 0, lhalo[...].astype(F32), 0.0)
    ext = jnp.concatenate([rim, load_ref[...].astype(F32)], axis=1)
    for p in range(NZ):
        ext_load[p] = ext[4 * p : 4 * p + 4]
    for lag in range(LAGS):
        stack[RANK * lag : RANK * (lag + 1)] = shifted_rows(ext, lag).astype(BF16)

    def first(j, carry):
        for copy in loads(j):
            copy.wait()
        rows = pl.ds(pl.multiple_of(j * TILE, TILE), TILE)
        recon = dot(pat[rows], stack[...])
        ratios[:, :SPAN] = (act[rows].astype(F32) / recon).astype(BF16)
        gram[...] += lax.dot_general(
            pat[rows], ratios[...], (((0,), (0,)), ((), ())), preferred_element_type=F32
        )
        return carry

    lax.fori_loop(0, TILES, first, 0)

    lane = lax.broadcasted_iota(jnp.int32, (RANK, HALO), 1)
    numer = jnp.zeros((RANK, EXT), F32)
    colsum = jnp.zeros((RANK, HALO), F32)
    for lag in range(LAGS):
        rows = gram[RANK * lag : RANK * (lag + 1)]
        wide = jnp.concatenate([jnp.zeros((RANK, HALO), F32), rows[:, :SPAN]], axis=1)
        numer = numer + (wide if lag == 0 else pltpu.roll(wide, EXT - lag, 1))
        colsum = colsum + rows[:, SPAN:]
    head = jnp.where(lane < 64, colsum, numer[:, :HALO])
    mine = jnp.concatenate([head, numer[:, HALO:]], axis=1)
    for p in range(NZ):
        blocks[0, p] = numer[4 * p : 4 * p + 4, :HALO]
        blocks[1, p] = numer[4 * p : 4 * p + 4, EXT - HALO :]
        part[p] = mine[4 * p : 4 * p + 4]

    edges = [
        remote(blocks.at[k, (z + d) % NZ], nhalo.at[k, d], EDGE + NZ * k + d, to, (z + d) % NZ)
        for k, to in enumerate((before, after))
        for d in range(NZ)
    ]
    for copy in edges:
        copy.start()

    def over_z(src, dst, base):
        return [remote(src(d), dst(d), base + d - 1, tm, (z + d) % NZ) for d in range(1, NZ)]

    scatter = over_z(lambda d: part.at[(z + d) % NZ], lambda d: zrecv.at[d - 1], ZRS)
    for copy in scatter:
        copy.start()
    for copy in scatter:
        copy.wait()
    total = part[z]
    for d in range(1, NZ):
        total = total + zrecv[d - 1]
    for copy in edges:
        copy.wait()
    near = [nhalo[k, 0] for k in range(2)]
    for d in range(1, NZ):
        near = [near[k] + nhalo[k, d] for k in range(2)]
    reach = lax.broadcasted_iota(jnp.int32, (4, HALO), 1) >= HALO - (LAGS - 1)
    from_after = jnp.where(reach & (tm < NTM - 1), near[0], 0.0)
    from_before = jnp.where(reach & (tm > 0), near[1], 0.0)
    total = jnp.concatenate(
        [total[:, :HALO] + from_before, total[:, HALO : EXT - HALO], total[:, EXT - HALO :] + from_after], axis=1
    )
    hz[z] = ext_load[z] * total / total[:, 0:1]
    gather = over_z(lambda d: hz.at[z], lambda d: hz.at[z], ZAG)
    for copy in gather:
        copy.start()
    for copy in gather:
        copy.wait()
    to_partner = remote(hz, hz_pair, HPAIR, partner, z)
    to_partner.start()

    def fresh_of(ref):
        return jnp.concatenate([ref[p] for p in range(NZ)], axis=0)

    h_ext = fresh_of(hz)
    h_ref[...] = h_ext[:, HALO:]

    def put_stack(full, direct, first_row):
        full = full.astype(BF16).astype(F32)
        for group in range(LAGS // 4):
            rows = [shifted_rows(full, 4 * group + k) for k in range(4)]
            block = jnp.concatenate(rows, axis=0)
            if direct:
                stack[4 * RANK * group : 4 * RANK * (group + 1)] = block.astype(BF16)
            turned = block.T
            stack_t[first_row : first_row + SPAN, HALO * group : HALO * (group + 1)] = turned.astype(BF16)
            lag_rows = jnp.broadcast_to(jnp.sum(turned, axis=0, keepdims=True), (8, HALO))
            if direct:
                lag8[group] = lag_rows
            else:
                lag8[group] = lag8[group] + lag_rows

    put_stack(h_ext, True, 0)
    sums[...] = jnp.zeros_like(sums)

    def pair_copy(i):
        return remote(rat.at[1 - c, i], prat.at[i], PAIR + i, partner, z)

    def make_ratio(i):
        dx, dy = relative(i)
        start = (((x + dx) % NX) * NY + (y + dy) % NY) * CROWS
        rows = pl.ds(pl.multiple_of(start, 16), CROWS)
        wide = act[rows].astype(F32)
        recon = dot(pat[rows], stack[...])
        ratio = wide / recon
        diverge = wide * jnp.log(ratio) - wide + recon
        sums[0] += jnp.sum(diverge.reshape(CROWS // 8, 8, SPAN), axis=0)
        sums[1] += jnp.sum(wide.reshape(CROWS // 8, 8, SPAN), axis=0)
        rat[0, i] = ratio[:OWN].astype(BF16)
        rat[1, i] = ratio[OWN:].astype(BF16)
        pair_copy(i).start()

    def ahead(i, carry):
        make_ratio(i)
        return carry

    lax.fori_loop(0, LEAD, ahead, 0)
    to_partner.wait()
    put_stack(fresh_of(hz_pair), False, SPAN)


    def half(i, step, other, block, base1, base2, recv1, recv2, plus, minus):
        @pl.when(step == 2)
        def _():
            for k, to in ((0, plus), (1, minus)):
                halved[i, block + k] = narrow(chunks[i, block + k])
                remote(halved.at[i, block + k], recv1.at[other, k], base1 + 2 * other + k, to, z).start()

        for k, (when, to) in enumerate(((1, plus), (3, minus))):

            @pl.when(step == when)
            def _():
                halved[i, block + 1 - k] = narrow(chunks[i, block + 1 - k])
                came = remote(halved.at[i, block], recv1.at[other, k], base1 + 2 * other + k, to, z)
                came.wait_recv()
                halved[i, block + k] = narrow(chunks[i, block + k] + widen(recv1[other, k]))
                remote(
                    halved.at[i, pl.ds(block, 2)], recv2.at[other, k], base2 + 2 * other + k, to, z
                ).start()

    def make_chunk(i):
        dx, dy = relative(i)
        pair_copy(i).wait_recv()
        made = dot(rat[c, i], stack_t[:SPAN]) + dot(prat[i], stack_t[SPAN:])
        for b in range(4):
            chunks[i, b, :OWN] = made[:, HALO * b : HALO * (b + 1)]
            chunks[i, b, OWN:] = lag8[b]
        half(i, dx, dy, 0, H1L, H2L, h1l, h2l, xp, xm)
        half(i, dy, dx, 2, H1R, H2R, h1r, h2r, yp, ym)

    def second(i, carry):
        make_ratio(i + LEAD)
        make_chunk(i)
        return carry

    def rest(i, carry):
        make_chunk(i)
        return carry

    def last_stage(pos, block, base2, recv2, cb1, cb2, crecv1, crecv2, plus, minus):
        def reduced(other):
            i = WHERE[pos(other)]
            for k in range(2):
                remote(
                    halved.at[i, pl.ds(block, 2)], recv2.at[other, k], base2 + 2 * other + k, plus, z
                ).wait_recv()
            for b in range(2):
                chunks[i, block + b] += widen(recv2[other, 0, b]) + widen(recv2[other, 1, b])
            return i

        def begin():
            i = reduced(2)
            remote(chunks.at[i, block], crecv1.at[0], cb1, plus, z).start()
            remote(chunks.at[i, block + 1], crecv1.at[1], cb1 + 1, minus, z).start()

        def middle():
            for k, (other, to) in enumerate(((1, plus), (3, minus))):
                i = reduced(other)
                remote(chunks.at[i, block], crecv1.at[k], cb1 + k, to, z).wait_recv()
                chunks[i, block + k] += crecv1[k]
                remote(chunks.at[i, pl.ds(block, 2)], crecv2.at[k], cb2 + k, to, z).start()

        def end():
            i = reduced(0)
            for k in range(2):
                remote(chunks.at[i, pl.ds(block, 2)], crecv2.at[k], cb2 + k, plus, z).wait_recv()
            chunks[i, pl.ds(block, 2)] = chunks[i, pl.ds(block, 2)] + crecv2[0] + crecv2[1]

        return begin, middle, end

    left = last_stage(lambda o: (0, o), 0, H2L, h2l, C1L, C2L, c1l, c2l, yp, ym)
    right = last_stage(lambda o: (o, 0), 2, H2R, h2r, C1R, C2R, c1r, c2r, xp, xm)
    lax.fori_loop(0, EARLY, second, 0)
    for begin in (left[0], right[0]):
        begin()
    lax.fori_loop(EARLY, CHUNKS - LEAD, second, 0)

    diverge = jnp.sum(sums[0], axis=0, keepdims=True)
    mass = jnp.sum(sums[1], axis=0, keepdims=True)
    row = lax.broadcasted_iota(jnp.int32, (8, SPAN), 0)
    zsums[0] = jnp.where(row == 0, diverge, mass)
    spread = over_z(lambda d: zsums.at[0], lambda d: zsums.at[d], ZMF)
    for copy in spread:
        copy.start()

    lax.fori_loop(CHUNKS - LEAD, CHUNKS - 1, rest, 0)
    for middle in (left[1], right[1]):
        middle()
    make_chunk(CHUNKS - 1)
    for end in (left[2], right[2]):
        end()


    mine = pl.ds(pl.multiple_of((x * NY + y) * CROWS, 16), CROWS)
    both = pat[mine].astype(F32)
    own = jnp.where(c == 0, both[:OWN], both[OWN:])
    for b in range(4):
        done = chunks[CHUNKS - 1, b]
        w_ref[:, HALO * b : HALO * (b + 1)] = own[:, HALO * b : HALO * (b + 1)] * done[:OWN] / done[OWN : OWN + 1]

    for copy in spread:
        copy.wait()
    everyone = zsums[0]
    for d in range(1, NZ):
        everyone = everyone + zsums[d]
    mis_ref[...] = everyone[0:1] / everyone[1:2]

    to_partner_done = [pair_copy(i) for i in range(CHUNKS)]
    for copy in to_partner_done:
        copy.wait_send()
    for base1, base2, recv1, recv2 in ((H1L, H2L, h1l, h2l), (H1R, H2R, h1r, h2r)):
        for other in range(4):
            for k in range(2):
                remote(halved.at[0, 0], recv1.at[other, k], base1 + 2 * other + k, xp, z).wait_send()
                remote(halved.at[0, pl.ds(0, 2)], recv2.at[other, k], base2 + 2 * other + k, xp, z).wait_send()
    for cb1, cb2, crecv1, crecv2 in ((C1L, C2L, c1l, c2l), (C1R, C2R, c1r, c2r)):
        for k in range(2):
            remote(chunks.at[0, 0], crecv1.at[k], cb1 + k, xp, z).wait_send()
            remote(chunks.at[0, pl.ds(0, 2)], crecv2.at[k], cb2 + k, xp, z).wait_send()


def body(activity, patterns, loadings):
    vmem = pl.BlockSpec(memory_space=pltpu.VMEM)
    anywhere = pl.BlockSpec(memory_space=pl.ANY)
    one = (PADDED, HALO)
    h_next, w_next, misfit = pl.pallas_call(
        kernel,
        out_shape=(
            jax.ShapeDtypeStruct((RANK, SPAN), F32),
            jax.ShapeDtypeStruct((OWN, WIDTH), F32),
            jax.ShapeDtypeStruct((1, SPAN), F32),
        ),
        in_specs=[anywhere, anywhere, vmem],
        out_specs=(vmem, vmem, vmem),
        scratch_shapes=[
            pltpu.VMEM((ROWS, SPAN), BF16),
            pltpu.VMEM((ROWS, WIDTH), BF16),
            pltpu.VMEM((WIDTH, SPAN), BF16),
            pltpu.VMEM((2 * SPAN, WIDTH), BF16),
            pltpu.VMEM((TILE, WIDTH), BF16),
            pltpu.VMEM((WIDTH, WIDTH), F32),
            pltpu.VMEM((RANK, HALO), BF16),
            pltpu.VMEM((2, NZ, 4, HALO), F32),
            pltpu.VMEM((2, NZ, 4, HALO), F32),
            pltpu.VMEM((NZ, 4, EXT), F32),
            pltpu.VMEM((NZ, 4, EXT), F32),
            pltpu.VMEM((NZ - 1, 4, EXT), F32),
            pltpu.VMEM((NZ, 4, EXT), F32),
            pltpu.VMEM((NZ, 4, EXT), F32),
            pltpu.VMEM((2, CHUNKS, OWN, SPAN), BF16),
            pltpu.VMEM((CHUNKS, OWN, SPAN), BF16),
            pltpu.VMEM((CHUNKS, 4) + one, F32),
            pltpu.VMEM((CHUNKS, 4) + one, BF16),
            pltpu.VMEM((4, 2) + one, BF16),
            pltpu.VMEM((4, 2, 2) + one, BF16),
            pltpu.VMEM((4, 2) + one, BF16),
            pltpu.VMEM((4, 2, 2) + one, BF16),
            pltpu.VMEM((2,) + one, F32),
            pltpu.VMEM((2, 2) + one, F32),
            pltpu.VMEM((2,) + one, F32),
            pltpu.VMEM((2, 2) + one, F32),
            pltpu.VMEM((2, 8, SPAN), F32),
            pltpu.VMEM((NZ, 8, SPAN), F32),
            pltpu.VMEM((4, 8, HALO), F32),
            pltpu.SemaphoreType.DMA((TILES, 2)),
            pltpu.SemaphoreType.DMA((NSEM,)),
            pltpu.SemaphoreType.DMA((NSEM,)),
        ],
        compiler_params=pltpu.CompilerParams(
            collective_id=0, has_side_effects=True, vmem_limit_bytes=60 * 1024 * 1024
        ),
    )(activity, patterns, loadings)
    return h_next, w_next, misfit.reshape(SPAN)


def solution(mesh):
    return jax.shard_map(
        body,
        mesh=mesh,
        in_specs=(P("neur", "tm"), P("neur", None), P(None, "tm")),
        out_specs=(P(None, "tm"), P(("neur", "tm"), None), P("tm")),
        check_vma=False,
    )
```
